32 devices in a mesh: batch: 4 (over z), neg: 2 (over y), weight: 4 (over x, core).
Axes of the slice: x: 2, y: 2, z: 4, core: 2. Of those that a mesh axis runs over, the one named last changes fastest.
Arguments:
- images: bfloat16 [1024, 2048], P('batch'), may hold values from -30 to 30
- img_pair: int32 [1024], P('batch'), may hold values from 0 to 1023, each once
- texts: bfloat16 [1024, 2048], P(('batch', 'neg', 'weight')), may hold values from -100 to 100
- txt_pair: int32 [1024], P(('batch', 'neg', 'weight')), may hold values from 0 to 1023, each once
- gain: float32 [2048], replicated, may hold values from 0.1 to 1.9
- perm: int32 [2048], replicated, may hold values from 0 to 2047, each once
- right_blocks: bfloat16 [32, 64, 64], P('weight'), may hold values from -0.75 to 0.75
- left_blocks: bfloat16 [32, 64, 64], P('weight'), may hold values from -0.75 to 0.75
Outputs:
- grad_img: bfloat16 [1024, 2048], P(('batch', 'neg', 'weight'))
- row_loss: float32 [1024], P('batch')
The draws below stay inside these ranges and needn't reach their ends.
Inputs may be any that keep to these rules, and one draw needn't show every extreme that they name: Every pair id appears once in img_pair and once in txt_pair.
All inputs are finite; a program needn't handle non-finite values.
Results may differ from the reference program's by a relative error of at most 0.0065.
Values may be sent and summed in bfloat16 or wider, within the bound.
A program may use at most 64 MiB of HBM per device.

```python
import math
import jax
import jax.numpy as jnp
from jax import lax

D = 2048
BS = 64
NB = 32
BATCH = 1024


def image_base(key):
    folded = jax.random.fold_in(key, 101)
    normal_key = jax.random.fold_in(folded, 0)
    values = jnp.clip(jax.random.normal(normal_key, (BATCH, D), jnp.float32), -6.0, 6.0)
    return values


def draw_images(key, part):
    values = image_base(key)
    return values.astype(jnp.bfloat16)


def draw_texts(key, part):
    own_key = jax.random.fold_in(key, 202)
    base_key = jax.random.fold_in(own_key, 0)
    return jnp.clip(jax.random.normal(base_key, (BATCH, D), jnp.float32), -6.0, 6.0).astype(jnp.bfloat16)


def level_of(key, dims, shards, low, largest):
    def one(position, shards_of):
        heights = jax.random.uniform(jax.random.fold_in(jax.random.fold_in(key, 6), position), (shards_of,), jnp.float32, low / len(shards), largest / len(shards))
        return jnp.repeat(jnp.exp(heights), dims[position] // shards_of).reshape((-1,) + (1,) * (len(dims) - position - 1))

    loudness = one(*shards[0])
    for cut in shards[1:]:
        loudness = loudness * one(*cut)
    return loudness


def gaussian(stream_key, shape, width, bound, cuts=(), dtype=jnp.bfloat16):
    result = width * jax.random.normal(stream_key, shape, jnp.float32)
    if cuts:
        result = result * level_of(stream_key, shape, cuts, -0.22, 0.18)
    return jnp.clip(result, -bound, bound).astype(dtype)


def setup_inputs(seed: int = 0) -> dict:
    key_list = jax.random.split(jax.random.key(seed), 9)
    images = draw_images(jax.random.fold_in(key_list[8], 71), 0)
    img_pair = jax.random.permutation(key_list[1], BATCH).astype(jnp.int32)
    texts = draw_texts(jax.random.fold_in(key_list[8], 71), 0)
    txt_pair = jax.random.permutation(key_list[3], BATCH).astype(jnp.int32)
    gain = jnp.clip(1.0 + 0.18 * jax.random.normal(key_list[4], (D,), jnp.float32), 0.1, 1.9)
    perm = jax.random.permutation(key_list[5], D).astype(jnp.int32)
    right_blocks = gaussian(key_list[6], (NB, BS, BS), BS ** -0.5, 0.75, ((0, 4),))
    left_blocks = gaussian(key_list[7], (NB, BS, BS), BS ** -0.5, 0.75, ((0, 4),))
    return dict(images=images, img_pair=img_pair, texts=texts, txt_pair=txt_pair, gain=gain, perm=perm, right_blocks=right_blocks, left_blocks=left_blocks)


LOGIT_GAIN = 2.8

def monarch(images, gain, perm, right_blocks, left_blocks):
    values = images.astype(jnp.float32)
    row_count = values.shape[0]
    row_mean = lax.optimization_barrier(jnp.mean(values, axis=1, keepdims=True))
    centered = values - row_mean
    row_var = lax.optimization_barrier(jnp.mean(centered * centered, axis=1, keepdims=True))
    normed = (centered * lax.rsqrt(row_var + 1e-05) * gain).astype(jnp.bfloat16)
    inner_mixed = jnp.einsum('rke,kec->rkc', normed.reshape(row_count, NB, BS).astype(jnp.float32), right_blocks.astype(jnp.float32))
    active = jax.nn.gelu(inner_mixed, approximate=True).astype(jnp.bfloat16).reshape(row_count, D)
    permuted = jnp.take(active, perm, axis=1)
    outer_mixed = jnp.einsum('rke,kec->rkc', permuted.reshape(row_count, NB, BS).astype(jnp.float32), left_blocks.astype(jnp.float32))
    return (values + outer_mixed.reshape(row_count, D)).astype(jnp.bfloat16)

def reference(images, img_pair, texts, txt_pair, gain, perm, right_blocks, left_blocks):
    logit_scale = LOGIT_GAIN / math.sqrt(D)
    blocks = 16
    row_count = BATCH // blocks

    def per_block(block_pair):
        image_rows, pair_rows = block_pair
        embedded = monarch(image_rows, gain, perm, right_blocks, left_blocks)
        scores = jnp.dot(embedded, texts.T, preferred_element_type=jnp.float32) * logit_scale
        matches = (pair_rows[:, None] == txt_pair[None, :]).astype(jnp.float32)
        row_max = lax.optimization_barrier(jnp.max(scores, axis=1))
        shifted = jnp.exp(scores - row_max[:, None])
        totals = lax.optimization_barrier(jnp.sum(shifted, axis=1))
        positive = lax.optimization_barrier(jnp.sum(matches * scores, axis=1))
        row_loss = row_max + jnp.log(totals) - positive
        dscore = (shifted / totals[:, None] - matches).astype(jnp.bfloat16)
        grads = jnp.dot(dscore, texts, preferred_element_type=jnp.float32).astype(jnp.bfloat16)
        return (grads, row_loss)
    grads, losses = lax.map(per_block, (images.reshape(blocks, row_count, D), img_pair.reshape(blocks, row_count)))
    return (grads.reshape(BATCH, D), losses.reshape(BATCH))
```

```python
import functools
import math

import jax
import jax.numpy as jnp
from jax import lax
from jax.experimental import pallas as pl
from jax.experimental.pallas import tpu as pltpu
from jax.sharding import PartitionSpec as P

LOGIT_GAIN = 2.8
MESH = pl.DeviceIdType.MESH
F32, BF16 = jnp.float32, jnp.bfloat16
PARTS = 2
VMEM_LIMIT = 67_043_328


def plane_orders(count):
    return [sorted(range(count), key=lambda o: (abs(o - own), o)) for own in range(count)]


def block_diagonal(wide):
    size = wide.shape[0]
    lane = lax.broadcasted_iota(jnp.int32, wide.shape, 1)
    values = wide.astype(F32)
    upper = jnp.where(lane < size, values, 0.0)
    lower = jnp.where(lane < size, 0.0, values)
    return jnp.concatenate([upper, lower], axis=0).astype(BF16)


def fused_kernel(
    dims, images_hbm, img_pair_hbm, texts_ref, txt_pair_hbm, gain_hbm, perm_hbm, right_hbm, left_hbm,
    grad_ref, loss_ref, img_pair_ref, txt_pair_ref, gain_ref, perm_ref, right_ref, left_ref,
    rows_ref, wts, buf, pairs, normed_ref, active_ref, permuted_ref, emb_ref, score_ref, dscore_ref, stats,
    partial_ref, peer_ref, own_ref,
    local_sem, wt_send, wt_recv, send_sem, recv_sem, pair_send, pair_recv, stat_send, stat_recv, part_send, part_recv,
):
    nb, nn, nw = dims
    width = texts_ref.shape[1]
    t_rows = texts_ref.shape[0]
    block_count, size = right_ref.shape[0], right_ref.shape[1]
    pair_count = block_count // 2
    lanes = 2 * size
    two = rows_ref.shape[0]
    r_rows = two // 2
    b, n, w = lax.axis_index("batch"), lax.axis_index("neg"), lax.axis_index("weight")
    core = lax.rem(w, 2)
    across = lax.div(w, 2)
    far = 1 - 2 * across
    flip = 1 - 2 * n
    n_a, w_a = n + core * flip, w + (1 - core) * 2 * far
    n_b, w_b = n + (1 - core) * flip, w + core * 2 * far
    n_d, w_d = 1 - n, w + 2 * far
    other = 1 - 2 * core
    w_p = w + other
    dev_a, dev_b, dev_p = (b, n_a, w_a), (b, n_b, w_b), (b, n, w_p)
    dev_ap = (b, n_a, w_a + other)
    dev_x = (b, n, w_d)
    dev_up, dev_down = (b + 1, n, w), (b - 1, n, w)
    me = n * nw + w
    side = core * n + (1 - core) * across
    spread = core * nw + (1 - core) * 2
    low = me - side * spread
    high = low + spread

    orders = plane_orders(nb)

    def by_plane(values):
        value = jnp.int32(values[0])
        for own in range(1, nb):
            value = jnp.where(b == own, values[own], value)
        return value

    planes = [by_plane([orders[own][k] for own in range(nb)]) for k in range(nb)]

    barrier = pltpu.get_barrier_semaphore()
    near = [dev_a, dev_b, dev_p, (b, n_d, w_d)]
    near += [dev_ap, (b, n_b, w_b + other), (b, n_d, w_d + other)]
    for dev in near:
        pl.semaphore_signal(barrier, inc=1, device_id=dev, device_id_type=MESH)

    @pl.when(b < nb - 1)
    def _():
        pl.semaphore_signal(barrier, inc=1, device_id=dev_up, device_id_type=MESH)

    @pl.when(b > 0)
    def _():
        pl.semaphore_signal(barrier, inc=1, device_id=dev_down, device_id_type=MESH)

    staged = [
        pltpu.make_async_copy(source, target, local_sem.at[3 + i])
        for i, (source, target) in enumerate([
            (right_hbm, right_ref), (left_hbm, left_ref), (txt_pair_hbm, txt_pair_ref),
            (gain_hbm, gain_ref), (perm_hbm, perm_ref), (img_pair_hbm, img_pair_ref),
        ])
    ]
    for copy in staged:
        copy.start()
    copy_rows = [
        pltpu.make_async_copy(
            images_hbm.at[pl.ds(pl.multiple_of(block * r_rows, r_rows), r_rows)],
            rows_ref.at[pl.ds(i * r_rows, r_rows)], local_sem.at[i],
        )
        for i, block in enumerate([low, high])
    ]
    copy_text = pltpu.make_async_copy(texts_ref, buf.at[b, 0], local_sem.at[2])
    for copy in copy_rows:
        copy.start()
    copy_text.start()
    expected = len(near) + jnp.where(b < nb - 1, 1, 0) + jnp.where(b > 0, 1, 0)
    pl.semaphore_wait(barrier, expected)

    def weight_copy(index, kind, dev):
        return pltpu.make_async_remote_copy(
            src_ref=wts.at[index], dst_ref=wts.at[index], send_sem=wt_send.at[kind], recv_sem=wt_recv.at[index],
            device_id=dev, device_id_type=MESH,
        )

    half = t_rows // PARTS

    targets = [(0, 3, dev_up), (0, 4, dev_down), (2, 0, dev_b), (3, 1, dev_ap), (1, 2, dev_p)]

    def text_copy(o, role, kind, part, dev, source):
        rows = pl.ds(pl.multiple_of(part * half, half), half)
        return pltpu.make_async_remote_copy(
            src_ref=source.at[rows], dst_ref=buf.at[o, role, rows], send_sem=send_sem.at[o, kind, part],
            recv_sem=recv_sem.at[o, role, part], device_id=dev, device_id_type=MESH,
        )

    def pair_copy(o, role, kind, dev):
        return pltpu.make_async_remote_copy(
            src_ref=pairs.at[o, 0], dst_ref=pairs.at[o, role], send_sem=pair_send.at[o, kind],
            recv_sem=pair_recv.at[o, role], device_id=dev, device_id_type=MESH,
        )

    sent = []

    def launch(copy, when):
        if when is None:
            copy.start()
            sent.append(copy.wait_send)
        else:
            pl.when(when)(copy.start)
            sent.append(lambda: pl.when(when)(copy.wait_send))

    def onward(kind, o):
        if kind == 3:
            return (o <= b) & (b < nb - 1)
        if kind == 4:
            return (o >= b) & (b > 0)
        return None

    def spread_text(o, part, source):
        for role, kind, dev in targets:
            launch(text_copy(o, role, kind, part, dev, source), onward(kind, o))

    def spread_pair(o):
        for role, kind, dev in targets:
            launch(pair_copy(o, role, kind, dev), onward(kind, o))

    def column(k, part):
        o = planes[k] if isinstance(k, int) else k
        text_copy(o, 0, 0, part, dev_b, buf.at[o, 0]).wait_recv()
        spread_text(o, part, buf.at[o, 0])

    def column_pair(k):
        o = planes[k]
        pair_copy(o, 0, 0, dev_b).wait_recv()
        spread_pair(o)

    def arrive(k):
        o = planes[k]
        for role in (1, 2, 3):
            for part in range(PARTS):
                text_copy(o, role, 0, part, dev_b, buf.at[o, 0]).wait_recv()
            pair_copy(o, role, 0, dev_b).wait_recv()

    for part in range(PARTS):
        spread_text(b, part, texts_ref)

    for copy in staged[:3]:
        copy.wait()
    pairs[b, 0] = jnp.concatenate([txt_pair_ref[...]] * 4, axis=1)
    for k in range(pair_count):
        wts[w, k] = jnp.concatenate([right_ref[2 * k], right_ref[2 * k + 1]], axis=1)
        wts[w, pair_count + k] = jnp.concatenate([left_ref[2 * k], left_ref[2 * k + 1]], axis=1)
    for copy in copy_rows:
        copy.wait()
    for copy in staged[3:]:
        copy.wait()
    weight_copy(w, 0, dev_x).start()
    weight_copy(w, 1, dev_p).start()
    spread_pair(b)

    values = rows_ref[...].astype(F32)
    mean = jnp.sum(values, axis=1, keepdims=True) / width
    centered = values - mean
    var = jnp.sum(centered * centered, axis=1, keepdims=True) / width
    normed_ref[...] = (centered * lax.rsqrt(var + 1e-05) * gain_ref[...]).astype(BF16)

    lane = lax.broadcasted_iota(jnp.int32, (two, img_pair_ref.shape[1]), 1)
    row = lax.broadcasted_iota(jnp.int32, (two, img_pair_ref.shape[1]), 0)
    place = lane == jnp.where(row < r_rows, low * r_rows + row, high * r_rows + row - r_rows)
    own_ids = jnp.sum(jnp.where(place, img_pair_ref[...], 0), axis=1, keepdims=True)

    def first_stage(s):
        for k in range(pair_count):
            at = pl.ds(pl.multiple_of((s * pair_count + k) * lanes, lanes), lanes)
            inner = jnp.dot(normed_ref[:, at], block_diagonal(wts[s, k]), preferred_element_type=F32)
            active_ref[:, at] = jax.nn.gelu(inner, approximate=True).astype(BF16)

    def second_stage(s):
        for k in range(pair_count):
            at = slice((s * pair_count + k) * lanes, (s * pair_count + k + 1) * lanes)
            outer = jnp.dot(
                permuted_ref[:, at], block_diagonal(wts[s, pair_count + k]), preferred_element_type=F32
            )
            emb_ref[:, at] = (rows_ref[:, at].astype(F32) + outer).astype(BF16)

    step = 2 * lanes
    row_id = lax.broadcasted_iota(jnp.int32, (width, step), 0)

    def permute(lo, hi):
        @pl.loop(lo, hi)
        def _(c):
            at = pl.ds(pl.multiple_of(c * step, step), step)
            chosen = jnp.where(row_id == perm_ref[:, at], 1.0, 0.0).astype(BF16)
            permuted_ref[:, at] = jnp.dot(active_ref[...], chosen, preferred_element_type=F32).astype(BF16)

    chunks = width // step
    middle = (b > 0) & (b < nb - 1)
    relays = [(k, part) for k in range(1, nb) for part in range(PARTS)]
    swapped = list(relays)
    if nb > 2 and PARTS == 2:
        swapped[1], swapped[2] = relays[2], relays[1]

    def relay(i):
        if i >= len(relays):
            return
        k, part = relays[i]
        if relays[i] == swapped[i]:
            column(k, part)
        else:
            k2, part2 = swapped[i]
            column(jnp.where(middle, planes[k2], planes[k]), jnp.where(middle, part2, part))

    first_stage(w)
    relay(0)
    weight_copy(w_p, 0, dev_x).wait_recv()
    first_stage(w_p)
    relay(1)
    relay(2)
    weight_copy(w_d, 0, dev_x).wait_recv()
    weight_copy(w_d, 2, dev_p).start()
    first_stage(w_d)
    relay(3)
    column_pair(1)
    w_dp = w_d + other
    weight_copy(w_dp, 0, dev_x).wait_recv()
    first_stage(w_dp)
    permute(0, chunks // 4)
    relay(4)
    permute(chunks // 4, chunks // 2)
    column_pair(2)
    relay(5)
    permute(chunks // 2, 3 * chunks // 4)
    for i in range(6, len(relays)):
        relay(i)
    for k in range(3, nb):
        column_pair(k)
    permute(3 * chunks // 4, chunks)
    for s in range(nw):
        second_stage(s)

    logit_scale = LOGIT_GAIN / math.sqrt(width)
    copy_text.wait()
    columns = 4 * t_rows

    def scores(k):
        if k:
            arrive(k)
        else:
            o = planes[0]
            for role in (1, 2, 3):
                for part in range(PARTS):
                    text_copy(o, role, 0, part, dev_b, buf.at[o, 0]).wait_recv()
                pair_copy(o, role, 0, dev_b).wait_recv()
        block = buf[planes[k]].reshape(columns, width)
        product = lax.dot_general(emb_ref[...], block, (((1,), (1,)), ((), ())), preferred_element_type=F32)
        score_ref[planes[k]] = product * logit_scale

    for k in range(nb):
        scores(k)

    quarter = lax.broadcasted_iota(jnp.int32, (1, columns), 1) // t_rows

    def pair_row(o):
        ids = pairs[o, 0]
        for role in range(1, 4):
            ids = jnp.where(quarter == role, pairs[o, role], ids)
        return ids

    found = [own_ids == pair_row(o) for o in range(nb)]
    parts = [score_ref[o] for o in range(nb)]
    row_max = jnp.max(functools.reduce(jnp.maximum, parts), axis=1, keepdims=True)
    totals = jnp.sum(
        functools.reduce(jnp.add, [jnp.exp(part - row_max) for part in parts]), axis=1, keepdims=True
    )
    positive = jnp.sum(
        functools.reduce(jnp.add, [jnp.where(hit, part, 0.0) for hit, part in zip(found, parts)]),
        axis=1, keepdims=True,
    )
    seat = lax.broadcasted_iota(jnp.int32, (two, stats.shape[2]), 0) == lax.broadcasted_iota(
        jnp.int32, (two, stats.shape[2]), 1
    )

    def to_row(value):
        return jnp.sum(jnp.where(seat, value, 0.0), axis=0, keepdims=True)

    def to_column(value):
        return jnp.sum(jnp.where(seat, value, 0.0), axis=1, keepdims=True)

    stats[me] = jnp.concatenate(
        [to_row(row_max), to_row(totals), to_row(positive), jnp.zeros((5, stats.shape[2]), F32)], axis=0
    )

    def stat_copy(index, position, dev):
        return pltpu.make_async_remote_copy(
            src_ref=stats.at[index], dst_ref=stats.at[index], send_sem=stat_send.at[position],
            recv_sem=stat_recv.at[index], device_id=dev, device_id_type=MESH,
        )

    for position, dev in enumerate(near):
        stat_copy(me, position, dev).start()
    peer = n_a * nw + w_a
    stat_copy(peer, 0, dev_a).wait_recv()
    theirs = stats[peer]
    peer_max = to_column(theirs[0:1])
    peer_totals = to_column(theirs[1:2])
    full_max = jnp.maximum(row_max, peer_max)
    full_totals = totals * jnp.exp(row_max - full_max) + peer_totals * jnp.exp(peer_max - full_max)
    for o in range(nb):
        dscore_ref[:, o * columns : (o + 1) * columns] = (
            jnp.exp(parts[o] - full_max) / full_totals - jnp.where(found[o], 1.0, 0.0)
        ).astype(BF16)

    tiles = partial_ref.shape[0]
    tile = width // tiles

    def gradient(first, c):
        block = buf[:, :, :, c * tile : (c + 1) * tile].reshape(nb * columns, tile)
        return jnp.dot(
            dscore_ref[pl.ds(pl.multiple_of(first, r_rows), r_rows)], block, preferred_element_type=F32
        )

    def part_copy(c):
        return pltpu.make_async_remote_copy(
            src_ref=partial_ref.at[c], dst_ref=peer_ref.at[c], send_sem=part_send.at[c],
            recv_sem=part_recv.at[c], device_id=dev_a, device_id_type=MESH,
        )

    for c in range(tiles):
        partial_ref[c] = gradient((1 - side) * r_rows, c).astype(BF16)
        part_copy(c).start()
    for c in range(tiles):
        own_ref[c] = gradient(side * r_rows, c)

    for _, n_o, w_o in near[1:]:
        stat_copy(n_o * nw + w_o, 0, dev_a).wait_recv()

    def pair_loss(one, two_):
        first, second = stats[one], stats[two_]
        top = jnp.maximum(first[0:1], second[0:1])
        total = first[1:2] * jnp.exp(first[0:1] - top) + second[1:2] * jnp.exp(second[0:1] - top)
        return top + jnp.log(total) - (first[2:3] + second[2:3])

    losses = {}
    for n_o in range(nn):
        both = pair_loss(n_o * nw, n_o * nw + 2)
        losses[n_o * nw], losses[n_o * nw + 2] = both[:, :r_rows], both[:, r_rows:two]
    for x_o in range(2):
        both = pair_loss(2 * x_o + 1, nw + 2 * x_o + 1)
        losses[2 * x_o + 1], losses[nw + 2 * x_o + 1] = both[:, :r_rows], both[:, r_rows:two]
    loss_ref[...] = jnp.concatenate([losses[i] for i in range(nn * nw)], axis=1)

    for c in range(tiles):
        part_copy(c).wait_recv()
        grad_ref[:, c * tile : (c + 1) * tile] = (own_ref[c] + peer_ref[c].astype(F32)).astype(BF16)

    for finish in sent:
        finish()
    weight_copy(w, 0, dev_x).wait_send()
    weight_copy(w, 1, dev_p).wait_send()
    weight_copy(w_d, 2, dev_p).wait_send()
    for position, dev in enumerate(near):
        stat_copy(me, position, dev).wait_send()
    for c in range(tiles):
        part_copy(c).wait_send()


def fused(dims, images, img_pair, texts, txt_pair, gain, perm, right_blocks, left_blocks):
    nb, nn, nw = dims
    group = nn * nw
    t_rows, width = texts.shape
    r_rows = images.shape[0] // group
    two = 2 * r_rows
    block_count, size = right_blocks.shape[:2]
    tiles = 4
    vmem = pl.BlockSpec(memory_space=pltpu.VMEM)
    hbm = pl.BlockSpec(memory_space=pltpu.HBM)
    dma = pltpu.SemaphoreType.DMA
    grad, loss = pl.pallas_call(
        functools.partial(fused_kernel, dims),
        out_shape=(
            jax.ShapeDtypeStruct((r_rows, width), BF16),
            jax.ShapeDtypeStruct((1, images.shape[0]), F32),
        ),
        in_specs=[hbm] * 8,
        out_specs=(vmem, vmem),
        scratch_shapes=[
            pltpu.VMEM((1, images.shape[0]), jnp.int32),
            pltpu.VMEM((1, t_rows), jnp.int32),
            pltpu.VMEM((1, width), F32),
            pltpu.VMEM((1, width), jnp.int32),
            pltpu.VMEM(right_blocks.shape, BF16),
            pltpu.VMEM(left_blocks.shape, BF16),
            pltpu.VMEM((two, width), BF16),
            pltpu.VMEM((nw, block_count, size, 2 * size), BF16),
            pltpu.VMEM((nb, 4, t_rows, width), BF16),
            pltpu.VMEM((nb, 4, 1, 4 * t_rows), jnp.int32),
            pltpu.VMEM((two, width), BF16),
            pltpu.VMEM((two, width), BF16),
            pltpu.VMEM((two, width), BF16),
            pltpu.VMEM((two, width), BF16),
            pltpu.VMEM((nb, two, 4 * t_rows), F32),
            pltpu.VMEM((two, nb * 4 * t_rows), BF16),
            pltpu.VMEM((group, 8, 128), F32),
            pltpu.VMEM((tiles, r_rows, width // tiles), BF16),
            pltpu.VMEM((tiles, r_rows, width // tiles), BF16),
            pltpu.VMEM((tiles, r_rows, width // tiles), F32),
            dma((9,)),
            dma((3,)),
            dma((nw,)),
            dma((nb, 5, PARTS)),
            dma((nb, 4, PARTS)),
            dma((nb, 5)),
            dma((nb, 4)),
            dma((group - 1,)),
            dma((group,)),
            dma((tiles,)),
            dma((tiles,)),
        ],
        compiler_params=pltpu.CompilerParams(
            collective_id=0, has_side_effects=True, vmem_limit_bytes=VMEM_LIMIT
        ),
    )(
        images, img_pair[None], texts, txt_pair[None], gain[None], perm[None], right_blocks, left_blocks
    )
    return grad, loss[0]


def monarch(images, gain, perm, right_full, left_full):
    row_count, width = images.shape
    block_count, block_size = (right_full.shape[0], right_full.shape[1])
    values = images.astype(jnp.float32)
    row_mean = jnp.mean(values, axis=1, keepdims=True)
    centered = values - row_mean
    row_var = jnp.mean(centered * centered, axis=1, keepdims=True)
    normed = (centered * lax.rsqrt(row_var + 1e-05) * gain).astype(jnp.bfloat16)
    inner_mixed = jnp.einsum(
        "rke,kec->rkc",
        normed.reshape(row_count, block_count, block_size),
        right_full,
        preferred_element_type=jnp.float32,
    )
    active = (
        jax.nn.gelu(inner_mixed, approximate=True).astype(jnp.bfloat16).reshape(row_count, width)
    )
    permuted = jnp.take(active, perm, axis=1)
    outer_mixed = jnp.einsum(
        "rke,kec->rkc",
        permuted.reshape(row_count, block_count, block_size),
        left_full,
        preferred_element_type=jnp.float32,
    )
    return (values + outer_mixed.reshape(row_count, width)).astype(jnp.bfloat16)


def per_device(images, img_pair, texts, txt_pair, gain, perm, right_blocks, left_blocks):
    right_full, left_full = (
        lax.all_gather(right_blocks, "weight", axis=0, tiled=True),
        lax.all_gather(left_blocks, "weight", axis=0, tiled=True),
    )
    embedded = monarch(images, gain, perm, right_full, left_full)
    gathered, gathered_pair = (
        lax.all_gather(texts, "batch", axis=0, tiled=True),
        lax.all_gather(txt_pair, "batch", axis=0, tiled=True),
    )
    logit_scale = LOGIT_GAIN / math.sqrt(images.shape[1])
    scores = (
        jnp.einsum("rd,cd->rc", embedded, gathered, preferred_element_type=jnp.float32)
        * logit_scale
    )
    matches = (img_pair[:, None] == gathered_pair[None, :]).astype(jnp.float32)
    local_max = jnp.max(scores, axis=1)
    local_pos = jnp.sum(matches * scores, axis=1)
    row_max = lax.pmax(local_max, ("neg", "weight"))
    shifted = jnp.exp(scores - row_max[:, None])
    totals, positive = lax.psum((jnp.sum(shifted, axis=1), local_pos), ("neg", "weight"))
    row_loss = row_max + jnp.log(totals) - positive
    dscore = (shifted / totals[:, None] - matches).astype(jnp.bfloat16)
    grad_sum = lax.psum_scatter(
        jnp.dot(dscore, gathered, preferred_element_type=jnp.float32),
        ("neg", "weight"),
        scatter_dimension=0,
        tiled=True,
    )
    grad_img = grad_sum.astype(jnp.bfloat16)
    return (grad_img, row_loss)


def solution(mesh):
    dims = tuple(mesh.shape[axis] for axis in ("batch", "neg", "weight"))

    def body(images, img_pair, texts, txt_pair, gain, perm, right_blocks, left_blocks):
        args = (images, img_pair, texts, txt_pair, gain, perm, right_blocks, left_blocks)
        rows = images.shape[0] // math.prod(dims[1:])
        if (
            dims[1:] == (2, 4) and 2 <= dims[0] <= 8 and texts.shape[0] == 16 * PARTS == rows
            and 2 * rows <= 128
        ):
            return fused(dims, *args)
        return per_device(*args)

    return jax.shard_map(
        body,
        mesh=mesh,
        in_specs=(
            P("batch", None),
            P("batch"),
            P(("batch", "neg", "weight"), None),
            P(("batch", "neg", "weight")),
            P(),
            P(),
            P("weight", None, None),
            P("weight", None, None),
        ),
        out_specs=(P(("batch", "neg", "weight"), None), P("batch")),
        check_vma=False,
    )
```

```python
import functools
import math

import jax
import jax.numpy as jnp
from jax import lax
from jax.experimental import pallas as pl
from jax.experimental.pallas import tpu as pltpu
from jax.sharding import PartitionSpec as P

LOGIT_GAIN = 2.8
MESH = pl.DeviceIdType.MESH
F32, BF16 = jnp.float32, jnp.bfloat16
PARTS = 2
VMEM_LIMIT = 48 * 2**20


def plane_orders(count):
    return [sorted(range(count), key=lambda o: (abs(o - own), o)) for own in range(count)]


def block_diagonal(wide):
    size = wide.shape[0]
    lane = lax.broadcasted_iota(jnp.int32, wide.shape, 1)
    values = wide.astype(F32)
    upper = jnp.where(lane < size, values, 0.0)
    lower = jnp.where(lane < size, 0.0, values)
    return jnp.concatenate([upper, lower], axis=0).astype(BF16)


def fused_kernel(
    dims, images_hbm, img_pair_hbm, texts_ref, txt_pair_hbm, gain_hbm, perm_hbm, right_hbm, left_hbm,
    grad_ref, loss_ref, img_pair_ref, txt_pair_ref, gain_ref, perm_ref, right_ref, left_ref,
    rows_ref, wts, buf, pairs, normed_ref, active_ref, permuted_ref, emb_ref, score_ref, dscore_ref, stats,
    partial_ref, peer_ref, own_ref,
    local_sem, wt_send, wt_recv, send_sem, recv_sem, pair_send, pair_recv, stat_send, stat_recv, part_send, part_recv,
):
    nb, nn, nw = dims
    width = texts_ref.shape[1]
    t_rows = texts_ref.shape[0]
    block_count, size = right_ref.shape[0], right_ref.shape[1]
    pair_count = block_count // 2
    lanes = 2 * size
    two = rows_ref.shape[0]
    r_rows = two // 2
    b, n, w = lax.axis_index("batch"), lax.axis_index("neg"), lax.axis_index("weight")
    core = lax.rem(w, 2)
    across = lax.div(w, 2)
    far = 1 - 2 * across
    flip = 1 - 2 * n
    n_a, w_a = n + core * flip, w + (1 - core) * 2 * far
    n_b, w_b = n + (1 - core) * flip, w + core * 2 * far
    n_d, w_d = 1 - n, w + 2 * far
    other = 1 - 2 * core
    w_p = w + other
    dev_a, dev_b, dev_p = (b, n_a, w_a), (b, n_b, w_b), (b, n, w_p)
    dev_ap = (b, n_a, w_a + other)
    dev_x = (b, n, w_d)
    dev_up, dev_down = (b + 1, n, w), (b - 1, n, w)
    me = n * nw + w
    side = core * n + (1 - core) * across
    spread = core * nw + (1 - core) * 2
    low = me - side * spread
    high = low + spread

    orders = plane_orders(nb)

    def by_plane(values):
        value = jnp.int32(values[0])
        for own in range(1, nb):
            value = jnp.where(b == own, values[own], value)
        return value

    planes = [by_plane([orders[own][k] for own in range(nb)]) for k in range(nb)]

    barrier = pltpu.get_barrier_semaphore()
    near = [dev_a, dev_b, dev_p, (b, n_d, w_d)]
    near += [dev_ap, (b, n_b, w_b + other), (b, n_d, w_d + other)]
    for dev in near:
        pl.semaphore_signal(barrier, inc=1, device_id=dev, device_id_type=MESH)

    @pl.when(b < nb - 1)
    def _():
        pl.semaphore_signal(barrier, inc=1, device_id=dev_up, device_id_type=MESH)

    @pl.when(b > 0)
    def _():
        pl.semaphore_signal(barrier, inc=1, device_id=dev_down, device_id_type=MESH)

    staged = [
        pltpu.make_async_copy(source, target, local_sem.at[3 + i])
        for i, (source, target) in enumerate([
            (right_hbm, right_ref), (left_hbm, left_ref), (txt_pair_hbm, txt_pair_ref),
            (gain_hbm, gain_ref), (perm_hbm, perm_ref), (img_pair_hbm, img_pair_ref),
        ])
    ]
    for copy in staged:
        copy.start()
    copy_rows = [
        pltpu.make_async_copy(
            images_hbm.at[pl.ds(pl.multiple_of(block * r_rows, r_rows), r_rows)],
            rows_ref.at[pl.ds(i * r_rows, r_rows)], local_sem.at[i],
        )
        for i, block in enumerate([low, high])
    ]
    copy_text = pltpu.make_async_copy(texts_ref, buf.at[b, 0], local_sem.at[2])
    for copy in copy_rows:
        copy.start()
    copy_text.start()
    expected = len(near) + jnp.where(b < nb - 1, 1, 0) + jnp.where(b > 0, 1, 0)
    pl.semaphore_wait(barrier, expected)

    def weight_copy(index, kind, dev):
        return pltpu.make_async_remote_copy(
            src_ref=wts.at[index], dst_ref=wts.at[index], send_sem=wt_send.at[kind], recv_sem=wt_recv.at[index],
            device_id=dev, device_id_type=MESH,
        )

    half = t_rows // PARTS

    targets = [(0, 3, dev_up), (0, 4, dev_down), (2, 0, dev_b), (3, 1, dev_ap), (1, 2, dev_p)]

    def text_copy(o, role, kind, part, dev, source):
        rows = pl.ds(pl.multiple_of(part * half, half), half)
        return pltpu.make_async_remote_copy(
            src_ref=source.at[rows], dst_ref=buf.at[o, role, rows], send_sem=send_sem.at[o, kind, part],
            recv_sem=recv_sem.at[o, role, part], device_id=dev, device_id_type=MESH,
        )

    def pair_copy(o, role, kind, dev):
        return pltpu.make_async_remote_copy(
            src_ref=pairs.at[o, 0], dst_ref=pairs.at[o, role], send_sem=pair_send.at[o, kind],
            recv_sem=pair_recv.at[o, role], device_id=dev, device_id_type=MESH,
        )

    sent = []

    def launch(copy, when):
        if when is None:
            copy.start()
            sent.append(copy.wait_send)
        else:
            pl.when(when)(copy.start)
            sent.append(lambda: pl.when(when)(copy.wait_send))

    def onward(kind, o):
        if kind == 3:
            return (o <= b) & (b < nb - 1)
        if kind == 4:
            return (o >= b) & (b > 0)
        return None

    def spread_text(o, part, source):
        for role, kind, dev in targets:
            launch(text_copy(o, role, kind, part, dev, source), onward(kind, o))

    def spread_pair(o):
        for role, kind, dev in targets:
            launch(pair_copy(o, role, kind, dev), onward(kind, o))

    def column(k, part):
        o = planes[k] if isinstance(k, int) else k
        text_copy(o, 0, 0, part, dev_b, buf.at[o, 0]).wait_recv()
        spread_text(o, part, buf.at[o, 0])

    def column_pair(k):
        o = planes[k]
        pair_copy(o, 0, 0, dev_b).wait_recv()
        spread_pair(o)

    def arrive(k):
        o = planes[k]
        for role in (1, 2, 3):
            for part in range(PARTS):
                text_copy(o, role, 0, part, dev_b, buf.at[o, 0]).wait_recv()
            pair_copy(o, role, 0, dev_b).wait_recv()

    for part in range(PARTS):
        spread_text(b, part, texts_ref)

    for copy in staged[:3]:
        copy.wait()
    pairs[b, 0] = jnp.concatenate([txt_pair_ref[...]] * 4, axis=1)
    for k in range(pair_count):
        wts[w, k] = jnp.concatenate([right_ref[2 * k], right_ref[2 * k + 1]], axis=1)
        wts[w, pair_count + k] = jnp.concatenate([left_ref[2 * k], left_ref[2 * k + 1]], axis=1)
    for copy in copy_rows:
        copy.wait()
    for copy in staged[3:]:
        copy.wait()
    weight_copy(w, 0, dev_x).start()
    weight_copy(w, 1, dev_p).start()
    spread_pair(b)

    values = rows_ref[...].astype(F32)
    mean = jnp.sum(values, axis=1, keepdims=True) / width
    centered = values - mean
    var = jnp.sum(centered * centered, axis=1, keepdims=True) / width
    normed_ref[...] = (centered * lax.rsqrt(var + 1e-05) * gain_ref[...]).astype(BF16)

    lane = lax.broadcasted_iota(jnp.int32, (two, img_pair_ref.shape[1]), 1)
    row = lax.broadcasted_iota(jnp.int32, (two, img_pair_ref.shape[1]), 0)
    place = lane == jnp.where(row < r_rows, low * r_rows + row, high * r_rows + row - r_rows)
    own_ids = jnp.sum(jnp.where(place, img_pair_ref[...], 0), axis=1, keepdims=True)

    def first_stage(s):
        for k in range(pair_count):
            at = pl.ds(pl.multiple_of((s * pair_count + k) * lanes, lanes), lanes)
            inner = jnp.dot(normed_ref[:, at], block_diagonal(wts[s, k]), preferred_element_type=F32)
            active_ref[:, at] = jax.nn.gelu(inner, approximate=True).astype(BF16)

    def second_stage(s):
        for k in range(pair_count):
            at = slice((s * pair_count + k) * lanes, (s * pair_count + k + 1) * lanes)
            outer = jnp.dot(
                permuted_ref[:, at], block_diagonal(wts[s, pair_count + k]), preferred_element_type=F32
            )
            emb_ref[:, at] = (rows_ref[:, at].astype(F32) + outer).astype(BF16)

    step = 2 * lanes
    row_id = lax.broadcasted_iota(jnp.int32, (width, step), 0)

    def permute(lo, hi):
        @pl.loop(lo, hi)
        def _(c):
            at = pl.ds(pl.multiple_of(c * step, step), step)
            chosen = jnp.where(row_id == perm_ref[:, at], 1.0, 0.0).astype(BF16)
            permuted_ref[:, at] = jnp.dot(active_ref[...], chosen, preferred_element_type=F32).astype(BF16)

    chunks = width // step
    middle = (b > 0) & (b < nb - 1)
    relays = [(k, part) for k in range(1, nb) for part in range(PARTS)]
    swapped = list(relays)
    if nb > 2 and PARTS == 2:
        swapped[1], swapped[2] = relays[2], relays[1]

    def relay(i):
        if i >= len(relays):
            return
        k, part = relays[i]
        if relays[i] == swapped[i]:
            column(k, part)
        else:
            k2, part2 = swapped[i]
            column(jnp.where(middle, planes[k2], planes[k]), jnp.where(middle, part2, part))

    first_stage(w)
    relay(0)
    weight_copy(w_p, 0, dev_x).wait_recv()
    first_stage(w_p)
    relay(1)
    relay(2)
    weight_copy(w_d, 0, dev_x).wait_recv()
    weight_copy(w_d, 2, dev_p).start()
    first_stage(w_d)
    relay(3)
    column_pair(1)
    w_dp = w_d + other
    weight_copy(w_dp, 0, dev_x).wait_recv()
    first_stage(w_dp)
    permute(0, chunks // 4)
    relay(4)
    permute(chunks // 4, chunks // 2)
    column_pair(2)
    relay(5)
    permute(chunks // 2, 3 * chunks // 4)
    for i in range(6, len(relays)):
        relay(i)
    for k in range(3, nb):
        column_pair(k)
    permute(3 * chunks // 4, chunks)
    for s in range(nw):
        second_stage(s)

    logit_scale = LOGIT_GAIN / math.sqrt(width)
    copy_text.wait()
    columns = 4 * t_rows

    def scores(k):
        if k:
            arrive(k)
        else:
            o = planes[0]
            for role in (1, 2, 3):
                for part in range(PARTS):
                    text_copy(o, role, 0, part, dev_b, buf.at[o, 0]).wait_recv()
                pair_copy(o, role, 0, dev_b).wait_recv()
        block = buf[planes[k]].reshape(columns, width)
        product = lax.dot_general(emb_ref[...], block, (((1,), (1,)), ((), ())), preferred_element_type=F32)
        score_ref[planes[k]] = product * logit_scale

    for k in range(nb):
        scores(k)

    quarter = lax.broadcasted_iota(jnp.int32, (1, columns), 1) // t_rows

    def pair_row(o):
        ids = pairs[o, 0]
        for role in range(1, 4):
            ids = jnp.where(quarter == role, pairs[o, role], ids)
        return ids

    found = [own_ids == pair_row(o) for o in range(nb)]
    parts = [score_ref[o] for o in range(nb)]
    row_max = jnp.max(functools.reduce(jnp.maximum, parts), axis=1, keepdims=True)
    totals = jnp.sum(
        functools.reduce(jnp.add, [jnp.exp(part - row_max) for part in parts]), axis=1, keepdims=True
    )
    positive = jnp.sum(
        functools.reduce(jnp.add, [jnp.where(hit, part, 0.0) for hit, part in zip(found, parts)]),
        axis=1, keepdims=True,
    )
    seat = lax.broadcasted_iota(jnp.int32, (two, stats.shape[2]), 0) == lax.broadcasted_iota(
        jnp.int32, (two, stats.shape[2]), 1
    )

    def to_row(value):
        return jnp.sum(jnp.where(seat, value, 0.0), axis=0, keepdims=True)

    def to_column(value):
        return jnp.sum(jnp.where(seat, value, 0.0), axis=1, keepdims=True)

    stats[me] = jnp.concatenate(
        [to_row(row_max), to_row(totals), to_row(positive), jnp.zeros((5, stats.shape[2]), F32)], axis=0
    )

    def stat_copy(index, position, dev):
        return pltpu.make_async_remote_copy(
            src_ref=stats.at[index], dst_ref=stats.at[index], send_sem=stat_send.at[position],
            recv_sem=stat_recv.at[index], device_id=dev, device_id_type=MESH,
        )

    for position, dev in enumerate(near):
        stat_copy(me, position, dev).start()
    peer = n_a * nw + w_a
    stat_copy(peer, 0, dev_a).wait_recv()
    theirs = stats[peer]
    peer_max = to_column(theirs[0:1])
    peer_totals = to_column(theirs[1:2])
    full_max = jnp.maximum(row_max, peer_max)
    full_totals = totals * jnp.exp(row_max - full_max) + peer_totals * jnp.exp(peer_max - full_max)
    for o in range(nb):
        dscore_ref[:, o * columns : (o + 1) * columns] = (
            jnp.exp(parts[o] - full_max) / full_totals - jnp.where(found[o], 1.0, 0.0)
        ).astype(BF16)

    tiles = partial_ref.shape[0]
    tile = width // tiles

    def gradient(first, c):
        block = buf[:, :, :, c * tile : (c + 1) * tile].reshape(nb * columns, tile)
        return jnp.dot(
            dscore_ref[pl.ds(pl.multiple_of(first, r_rows), r_rows)], block, preferred_element_type=F32
        )

    def part_copy(c):
        return pltpu.make_async_remote_copy(
            src_ref=partial_ref.at[c], dst_ref=peer_ref.at[c], send_sem=part_send.at[c],
            recv_sem=part_recv.at[c], device_id=dev_a, device_id_type=MESH,
        )

    for c in range(tiles):
        partial_ref[c] = gradient((1 - side) * r_rows, c).astype(BF16)
        part_copy(c).start()
    for c in range(tiles):
        own_ref[c] = gradient(side * r_rows, c)

    for _, n_o, w_o in near[1:]:
        stat_copy(n_o * nw + w_o, 0, dev_a).wait_recv()

    def pair_loss(one, two_):
        first, second = stats[one], stats[two_]
        top = jnp.maximum(first[0:1], second[0:1])
        total = first[1:2] * jnp.exp(first[0:1] - top) + second[1:2] * jnp.exp(second[0:1] - top)
        return top + jnp.log(total) - (first[2:3] + second[2:3])

    losses = {}
    for n_o in range(nn):
        both = pair_loss(n_o * nw, n_o * nw + 2)
        losses[n_o * nw], losses[n_o * nw + 2] = both[:, :r_rows], both[:, r_rows:two]
    for x_o in range(2):
        both = pair_loss(2 * x_o + 1, nw + 2 * x_o + 1)
        losses[2 * x_o + 1], losses[nw + 2 * x_o + 1] = both[:, :r_rows], both[:, r_rows:two]
    loss_ref[...] = jnp.concatenate([losses[i] for i in range(nn * nw)], axis=1)[0]

    for c in range(tiles):
        part_copy(c).wait_recv()
        grad_ref[:, c * tile : (c + 1) * tile] = (own_ref[c] + peer_ref[c].astype(F32)).astype(BF16)

    for finish in sent:
        finish()
    weight_copy(w, 0, dev_x).wait_send()
    weight_copy(w, 1, dev_p).wait_send()
    weight_copy(w_d, 2, dev_p).wait_send()
    for position, dev in enumerate(near):
        stat_copy(me, position, dev).wait_send()
    for c in range(tiles):
        part_copy(c).wait_send()


def fused(dims, images, img_pair, texts, txt_pair, gain, perm, right_blocks, left_blocks):
    nb, nn, nw = dims
    group = nn * nw
    t_rows, width = texts.shape
    r_rows = images.shape[0] // group
    two = 2 * r_rows
    block_count, size = right_blocks.shape[:2]
    tiles = 4
    vmem = pl.BlockSpec(memory_space=pltpu.VMEM)
    hbm = pl.BlockSpec(memory_space=pltpu.HBM)
    dma = pltpu.SemaphoreType.DMA
    grad, loss = pl.pallas_call(
        functools.partial(fused_kernel, dims),
        out_shape=(
            jax.ShapeDtypeStruct((r_rows, width), BF16),
            jax.ShapeDtypeStruct((images.shape[0],), F32),
        ),
        in_specs=[hbm] * 8,
        out_specs=(vmem, vmem),
        scratch_shapes=[
            pltpu.VMEM((1, images.shape[0]), jnp.int32),
            pltpu.VMEM((1, t_rows), jnp.int32),
            pltpu.VMEM((1, width), F32),
            pltpu.VMEM((1, width), jnp.int32),
            pltpu.VMEM(right_blocks.shape, BF16),
            pltpu.VMEM(left_blocks.shape, BF16),
            pltpu.VMEM((two, width), BF16),
            pltpu.VMEM((nw, block_count, size, 2 * size), BF16),
            pltpu.VMEM((nb, 4, t_rows, width), BF16),
            pltpu.VMEM((nb, 4, 1, 4 * t_rows), jnp.int32),
            pltpu.VMEM((two, width), BF16),
            pltpu.VMEM((two, width), BF16),
            pltpu.VMEM((two, width), BF16),
            pltpu.VMEM((two, width), BF16),
            pltpu.VMEM((nb, two, 4 * t_rows), F32),
            pltpu.VMEM((two, nb * 4 * t_rows), BF16),
            pltpu.VMEM((group, 8, 128), F32),
            pltpu.VMEM((tiles, r_rows, width // tiles), BF16),
            pltpu.VMEM((tiles, r_rows, width // tiles), BF16),
            pltpu.VMEM((tiles, r_rows, width // tiles), F32),
            dma((9,)),
            dma((3,)),
            dma((nw,)),
            dma((nb, 5, PARTS)),
            dma((nb, 4, PARTS)),
            dma((nb, 5)),
            dma((nb, 4)),
            dma((group - 1,)),
            dma((group,)),
            dma((tiles,)),
            dma((tiles,)),
        ],
        compiler_params=pltpu.CompilerParams(
            collective_id=0, has_side_effects=True, vmem_limit_bytes=VMEM_LIMIT
        ),
    )(
        *[
            pltpu.with_memory_space_constraint(value, pltpu.HBM)
            for value in (images, img_pair[None], texts, txt_pair[None], gain[None], perm[None], right_blocks, left_blocks)
        ]
    )
    return pl.pallas_call(
        hand_out,
        out_shape=(
            jax.ShapeDtypeStruct((r_rows, width), BF16),
            jax.ShapeDtypeStruct((images.shape[0],), F32),
        ),
        in_specs=[vmem, vmem],
        out_specs=(hbm, hbm),
        scratch_shapes=[dma((2,))],
        compiler_params=pltpu.CompilerParams(vmem_limit_bytes=2**20),
    )(grad, loss)


def hand_out(grad_ref, loss_ref, grad_hbm, loss_hbm, sem):
    copies = [
        pltpu.make_async_copy(grad_ref, grad_hbm, sem.at[0]),
        pltpu.make_async_copy(loss_ref, loss_hbm, sem.at[1]),
    ]
    for copy in copies:
        copy.start()
    for copy in copies:
        copy.wait()


def monarch(images, gain, perm, right_full, left_full):
    row_count, width = images.shape
    block_count, block_size = (right_full.shape[0], right_full.shape[1])
    values = images.astype(jnp.float32)
    row_mean = jnp.mean(values, axis=1, keepdims=True)
    centered = values - row_mean
    row_var = jnp.mean(centered * centered, axis=1, keepdims=True)
    normed = (centered * lax.rsqrt(row_var + 1e-05) * gain).astype(jnp.bfloat16)
    inner_mixed = jnp.einsum(
        "rke,kec->rkc",
        normed.reshape(row_count, block_count, block_size),
        right_full,
        preferred_element_type=jnp.float32,
    )
    active = (
        jax.nn.gelu(inner_mixed, approximate=True).astype(jnp.bfloat16).reshape(row_count, width)
    )
    permuted = jnp.take(active, perm, axis=1)
    outer_mixed = jnp.einsum(
        "rke,kec->rkc",
        permuted.reshape(row_count, block_count, block_size),
        left_full,
        preferred_element_type=jnp.float32,
    )
    return (values + outer_mixed.reshape(row_count, width)).astype(jnp.bfloat16)


def per_device(images, img_pair, texts, txt_pair, gain, perm, right_blocks, left_blocks):
    right_full, left_full = (
        lax.all_gather(right_blocks, "weight", axis=0, tiled=True),
        lax.all_gather(left_blocks, "weight", axis=0, tiled=True),
    )
    embedded = monarch(images, gain, perm, right_full, left_full)
    gathered, gathered_pair = (
        lax.all_gather(texts, "batch", axis=0, tiled=True),
        lax.all_gather(txt_pair, "batch", axis=0, tiled=True),
    )
    logit_scale = LOGIT_GAIN / math.sqrt(images.shape[1])
    scores = (
        jnp.einsum("rd,cd->rc", embedded, gathered, preferred_element_type=jnp.float32)
        * logit_scale
    )
    matches = (img_pair[:, None] == gathered_pair[None, :]).astype(jnp.float32)
    local_max = jnp.max(scores, axis=1)
    local_pos = jnp.sum(matches * scores, axis=1)
    row_max = lax.pmax(local_max, ("neg", "weight"))
    shifted = jnp.exp(scores - row_max[:, None])
    totals, positive = lax.psum((jnp.sum(shifted, axis=1), local_pos), ("neg", "weight"))
    row_loss = row_max + jnp.log(totals) - positive
    dscore = (shifted / totals[:, None] - matches).astype(jnp.bfloat16)
    grad_sum = lax.psum_scatter(
        jnp.dot(dscore, gathered, preferred_element_type=jnp.float32),
        ("neg", "weight"),
        scatter_dimension=0,
        tiled=True,
    )
    grad_img = grad_sum.astype(jnp.bfloat16)
    return (grad_img, row_loss)


def solution(mesh):
    dims = tuple(mesh.shape[axis] for axis in ("batch", "neg", "weight"))

    def body(images, img_pair, texts, txt_pair, gain, perm, right_blocks, left_blocks):
        args = (images, img_pair, texts, txt_pair, gain, perm, right_blocks, left_blocks)
        rows = images.shape[0] // math.prod(dims[1:])
        if (
            dims[1:] == (2, 4) and 2 <= dims[0] <= 8 and texts.shape[0] == 16 * PARTS == rows
            and 2 * rows <= 128
        ):
            return fused(dims, *args)
        return per_device(*args)

    return jax.shard_map(
        body,
        mesh=mesh,
        in_specs=(
            P("batch", None),
            P("batch"),
            P(("batch", "neg", "weight"), None),
            P(("batch", "neg", "weight")),
            P(),
            P(),
            P("weight", None, None),
            P("weight", None, None),
        ),
        out_specs=(P(("batch", "neg", "weight"), None), P("batch")),
        check_vma=False,
    )
```
